256 devices in a mesh: users: 32 (over y, z_lo, core), heads: 8 (over x, z_hi).
Axes of the slice: x: 4, y: 4, z: 8 (z_hi: 2, z_lo: 4; z = z_hi * 4 + z_lo), core: 2. Of those that a mesh axis runs over, the one named last changes fastest.
Arguments:
- sessions: bfloat16 [65536, 4096], P(('users', 'heads')), parts along dimension 0, may hold values from -16 to 16
- input_weight: bfloat16 [3, 4096, 2048], P(None, None, 'heads'), may hold values from -1 to 1
- output_weight: bfloat16 [2048, 4096], P('heads'), may hold values from -0.359375 to 0.359375
- session_counts: int32 [64], P('users'), parts along dimension 0, may hold values from 1 to 1536, 2048 in all
Outputs:
- attended: bfloat16 [65536, 4096], P(('users', 'heads')), parts along dimension 0
The draws below stay inside these ranges and needn't reach their ends.
There are 32 independent parts, one for each index of `users`. The reference program is written for one: setup_inputs(seed, part) draws one part's arguments, and reference() takes and returns one part's arrays. A program takes and returns all parts, laid end to end along the dimension named above; an argument that names none is the same for every part. Nothing has to cross between parts.
Inputs may be any that keep to these rules, and one draw needn't show every extreme that they name: `session_counts`: the 2 counts sum to 2048.
All inputs are finite; a program needn't handle non-finite values.
Results may differ from the reference program's by a relative error of at most 0.015.
Values may be sent and summed in bfloat16 or wider, within the bound.
A program may use at most 128 MiB of HBM per device.

```python
import math
import jax
import jax.numpy as jnp
import numpy as np
from jax import lax

D = 4096
HEADS = 16
HD = 128
HIST = 2
SESSIONS = 2048
N_HEADS = 8


def draw_sessions(key, part):
    key_base = jax.random.fold_in(key, 0)
    result = jax.random.truncated_normal(key_base, -6.0, 6.0, (SESSIONS, D), jnp.float32)
    return result.astype(jnp.bfloat16)


def draw_input_weight(key, part):
    key_first, key_second, key_third = jax.random.split(key, 3)
    shape = (D, HEADS * HD)
    factor = D ** (-0.5)
    query_part = jax.random.truncated_normal(key_first, -6.0, 6.0, shape, jnp.float32) * factor
    key_part = jax.random.truncated_normal(key_second, -6.0, 6.0, shape, jnp.float32) * factor
    value_part = jax.random.truncated_normal(key_third, -6.0, 6.0, shape, jnp.float32) * factor
    return jnp.stack([query_part, key_part, value_part]).astype(jnp.bfloat16)


def steps_of(rng, extent, pieces, low, high):
    loudness, own = 1.0, jax.random.fold_in(rng, 6)
    for dim, parts in pieces:
        heights = jnp.exp(jax.random.uniform(jax.random.fold_in(own, dim), (parts,), jnp.float32, low / len(pieces), high / len(pieces)))
        loudness = loudness * jnp.repeat(heights, extent[dim] // parts).reshape([-1 if axis == dim else 1 for axis in range(len(extent))])
    return loudness


def profile(number_of, total, most, slope):
    weights = [(1 << 20) // math.isqrt(grade ** slope) + 1 for grade in range(2, number_of + 1)]
    spare, given = total - most - (number_of - 1), [1] * (number_of - 1)
    while spare > 0:
        free = [i for i in range(number_of - 1) if given[i] < most]
        pool, remaining = sum([weights[i] for i in free]), spare
        for i in free:
            addition = min(most - given[i], max(1, remaining * weights[i] // pool), spare)
            given[i] = given[i] + addition
            spare = spare - addition
    return np.array([most] + given)


def uneven_parts(stream_key, number_of, total, limit, lean):
    if number_of == 2:
        one = jax.random.randint(stream_key, (), max(1, total - limit), min(limit, total - 1) + 1)
        return jnp.stack([one, total - one])
    sizes = jnp.asarray(profile(number_of, total, limit, lean), jnp.int32)
    couples = (number_of - 1) // 2
    source_of, receiver = sizes[1:1 + 2 * couples:2], sizes[2:2 + 2 * couples:2]
    slack = jnp.minimum(source_of - 1, limit - receiver)
    passed = jax.random.randint(jax.random.fold_in(stream_key, 1), (couples,), 0, 1 << 20) % (slack + 1)
    sizes = sizes.at[1:1 + 2 * couples:2].set(source_of - passed).at[2:2 + 2 * couples:2].set(receiver + passed)
    return sizes[jax.random.permutation(jax.random.fold_in(stream_key, 2), number_of)]


def normal_values(rng, extent, spread, most, shards=(), held_as=jnp.bfloat16):
    factor_of = steps_of(rng, extent, shards, -0.22, 0.18) if shards else 1.0
    entries = jax.random.normal(rng, extent, jnp.float32) * spread * factor_of
    return jnp.minimum(jnp.maximum(entries, -most), most).astype(held_as)


def setup_inputs(seed: int = 0, part: int = 0) -> dict:
    key_list = jax.random.split(jax.random.key(seed), 5)
    part_splits = jax.random.split(jax.random.fold_in(key_list[4], part), 5)
    return {
        "sessions": draw_sessions(jax.random.fold_in(jax.random.fold_in(key_list[4], part), 71), part),
        "input_weight": draw_input_weight(jax.random.fold_in(key_list[4], 71), part),
        "output_weight": normal_values(key_list[2], (HEADS * HD, D), 0.06, 0.359375, ((0, 8),)),
        "session_counts": uneven_parts(part_splits[3], HIST, SESSIONS, SESSIONS * 3 // 4, 2).astype(jnp.int32),
    }


def permitted(total, counts):
    positions = jnp.arange(total, dtype=jnp.int32)
    ends = jnp.cumsum(counts).astype(jnp.int32)
    row_user = jnp.sum((positions[:, None] >= ends[None, :]).astype(jnp.int32), axis=1)
    same_user = row_user[:, None] == row_user[None, :]
    return jnp.logical_and(same_user, positions[:, None] >= positions[None, :])


def attend(packed, allowed):
    total = packed.shape[1]
    width = packed.shape[2]
    queries = packed[0].reshape(total, width // HD, HD).astype(jnp.float32)
    key_rows = packed[1].reshape(total, width // HD, HD).astype(jnp.float32)
    values = packed[2].reshape(total, width // HD, HD).astype(jnp.float32)
    scores = jnp.einsum("qhe,khe->hqk", queries, key_rows) * (HD ** -0.5)
    scores = jnp.where(allowed[None], scores, -1e30)
    highest = jnp.max(scores, axis=2, keepdims=True)
    raised = jnp.where(allowed[None], jnp.exp(scores - highest), 0.0)
    attn_probs = (raised / jnp.sum(raised, axis=2, keepdims=True)).astype(jnp.bfloat16)
    mixed = jnp.einsum("hqk,khe->qhe", attn_probs.astype(jnp.float32), values)
    return mixed.astype(jnp.bfloat16).reshape(total, width)


def reference(sessions, input_weight, output_weight, session_counts):
    total = sessions.shape[0]
    allowed = permitted(total, session_counts)
    packed = jnp.einsum("nd,cde->cne", sessions.astype(jnp.float32), input_weight.astype(jnp.float32)).astype(jnp.bfloat16)
    group_width = HEADS * HD // N_HEADS

    def one_group(running, index):
        begin = (index * group_width).astype(jnp.int32)
        part_cols = lax.dynamic_slice_in_dim(packed, begin, group_width, 2)
        mixed = attend(part_cols, allowed)
        weight_rows = lax.dynamic_slice_in_dim(output_weight, begin, group_width, 0)
        partial_value = jnp.dot(mixed, weight_rows, preferred_element_type=jnp.float32).astype(jnp.bfloat16)
        partial_value = lax.optimization_barrier(partial_value)
        return running + partial_value.astype(jnp.float32), None

    start_sum = jnp.zeros((total, sessions.shape[1]), jnp.float32)
    result, unused = lax.scan(one_group, start_sum, jnp.arange(N_HEADS, dtype=jnp.int32))
    return result.astype(jnp.bfloat16)
```

```python
import jax
import jax.numpy as jnp
from jax import lax
from jax.experimental import pallas as pl
from jax.experimental.pallas import tpu as pltpu
from jax.sharding import PartitionSpec as P

HD = 128
D = 4096
ROWS = 256
HALF = 128
TOTAL = 2048
COLS = 256
MESH = pl.DeviceIdType.MESH

ZX = 0
R1P, R1M = 2, 4
R2P, R2M = 6, 7
SX = 8
WZ = 16
WYP, WYM, WY2 = 20, 23, 26
WXP, WXM, WX2 = 29, 30, 31
V1P, V1M = 32, 34
V2P, V2M = 36, 37
SV = 38
CN = 46
NCOPY = 47


def place(x, y, z, c):
    x, y, z, c = (lax.rem(x + 4, 4), lax.rem(y + 4, 4), lax.rem(z + 8, 8), lax.rem(c, 2))
    return ((y * 4 + lax.rem(z, 4)) * 2 + c, x * 2 + z // 4)


def kernel(
    cnt_ref, x_hbm, w_hbm, v_hbm, out_hbm,
    xg, wq, vg, qkv, obuf, mix, obf, cnt,
    ssem, rsem, osend, orecv, lsem, outsem,
):
    u, h = lax.axis_index("users"), lax.axis_index("heads")
    x, s, y, zl, c = h // 2, lax.rem(h, 2), u // 8, lax.rem(u // 2, 4), lax.rem(u, 2)
    z = s * 4 + zl
    native = c == s
    foreign = c != s
    edge = jnp.logical_or(zl == 0, zl == 3)
    dz_out = jnp.where(zl >= 2, 1, 7)
    dz_in = jnp.where(zl >= 2, 7, 1)
    xm, xp, x2 = lax.rem(x + 3, 4), lax.rem(x + 1, 4), lax.rem(x + 2, 4)
    ym, yp, y2 = lax.rem(y + 3, 4), lax.rem(y + 1, 4), lax.rem(y + 2, 4)
    sib = place(x, y, z, c + 1)
    to_xp, to_xm, to_x2 = place(xp, y, z, c), place(xm, y, z, c), place(x2, y, z, c)
    to_yp, to_ym, to_y2 = place(x, yp, z, c), place(x, ym, z, c), place(x, y2, z, c)
    across = place(x, y, z + 4, c + 1)
    outer = place(x, y, z + dz_out, c)
    inner = place(x, y, z + dz_in, c)

    def copy(i, src, dst, target):
        return pltpu.make_async_remote_copy(
            src_ref=src, dst_ref=dst, send_sem=ssem.at[i], recv_sem=rsem.at[i],
            device_id=target, device_id_type=MESH,
        )

    def send(i, ref, target):
        copy(i, ref, ref, target).start()

    def got(i, ref):
        copy(i, ref, ref, sib).wait_recv()

    def sent(i, ref):
        copy(i, ref, ref, sib).wait_send()

    def xh(bx, bp, half):
        return xg.at[bx, bp, half]

    def vlo(by):
        return vg.at[pl.ds(0, 2), c, by]

    def vhi(by):
        return vg.at[pl.ds(2, 2), c, by]

    def wpart(ref, m):
        return ref.at[m, pl.ds(pl.multiple_of(y * 1024, 1024), 1024)]

    vmine = vg.at[x, c, y]
    quarter = v_hbm.at[pl.ds(pl.multiple_of(y * 64, 64), 64)]

    load_x = [
        pltpu.make_async_copy(x_hbm.at[pl.ds(HALF * i, HALF)], xh(x, c, i), lsem.at[i])
        for i in range(2)
    ]
    load_w = pltpu.make_async_copy(w_hbm, wq, lsem.at[2])
    load_v = pltpu.make_async_copy(quarter, vmine, lsem.at[3])

    @pl.when(native)
    def _():
        load_v.start()
        for cp in load_x:
            cp.start()
        load_w.start()
        cnt[...] = jnp.full(cnt.shape, cnt_ref[0], jnp.int32)

    barrier = pltpu.get_barrier_semaphore()
    peers = [place(x + dx, y, z + dz, c + dc) for dx in range(4) for dz in (0, 4) for dc in (0, 1)][1:]
    peers += [to_yp, to_ym, to_y2, place(x, y, z + 1, c), place(x, y, z + 7, c)]
    for peer in peers:
        pl.semaphore_signal(barrier, inc=1, device_id=peer, device_id_type=MESH)
    pl.semaphore_wait(barrier, len(peers))

    def share_v():
        send(WXP, vmine, to_xp)
        send(WXM, vmine, to_xm)
        send(WX2, vmine, to_x2)

    def first_a():
        send(R1P, xh(x, c, 0), to_xp)
        send(R1M, xh(x, c, 0), to_xm)
        send(SX, xh(x, c, 0), sib)

    def first_b():
        send(R1P + 1, xh(x, c, 1), to_xp)
        send(R1M + 1, xh(x, c, 1), to_xm)
        send(SX + 1, xh(x, c, 1), sib)

    def bundle():
        for i in (WXP, WXM, WX2):
            got(i, vmine)
        send(V1P, vlo(y), to_yp)
        send(V1M + 1, vhi(y), to_ym)
        send(V1P + 1, vhi(y), to_yp)
        send(V1M, vlo(y), to_ym)
        send(SV, vlo(y), sib)
        send(SV + 1, vhi(y), sib)

    def bundle_on():
        got(V1P, vlo(ym))
        send(V2P, vlo(ym), to_yp)
        send(SV + 2, vlo(ym), sib)
        got(V1M + 1, vhi(yp))
        send(V2M, vhi(yp), to_ym)
        send(SV + 5, vhi(yp), sib)
        got(V1P + 1, vhi(ym))
        send(SV + 3, vhi(ym), sib)
        got(V1M, vlo(yp))
        send(SV + 4, vlo(yp), sib)

    @pl.when(native)
    def _():
        @pl.when(edge)
        def _():
            copy(WZ + 3, quarter, vmine, outer).start()
            for m in range(3):
                copy(WZ + m, wpart(w_hbm, m), wpart(wq, m), outer).start()

        send(CN, cnt, sib)
        load_v.wait()
        share_v()
        for cp in load_x:
            cp.wait()
        first_a()
        first_b()
        bundle()

    @pl.when(foreign)
    def _():
        for i in range(2):
            copy(ZX + i, x_hbm.at[pl.ds(HALF * i, HALF)], xh(x, 1 - c, i), across).start()

        def relay(i, ref):
            got(i, ref)

            @pl.when(edge)
            def _():
                send(i, ref, inner)

        def spread(m):
            relay(WZ + m, wpart(wq, m))
            send(WYP + m, wpart(wq, m), to_yp)
            send(WYM + m, wpart(wq, m), to_ym)
            send(WY2 + m, wpart(wq, m), to_y2)

        relay(WZ + 3, vmine)
        share_v()
        spread(0)
        got(ZX, xh(x, c, 0))
        first_a()
        spread(1)
        spread(2)
        got(ZX + 1, xh(x, c, 1))
        first_b()

    got(R1P, xh(xm, c, 0))
    send(R2P, xh(xm, c, 0), to_xp)
    send(SX + 2, xh(xm, c, 0), sib)
    got(R1M + 1, xh(xp, c, 1))
    send(R2M, xh(xp, c, 1), to_xm)
    send(SX + 5, xh(xp, c, 1), sib)
    got(R1P + 1, xh(xm, c, 1))
    send(SX + 3, xh(xm, c, 1), sib)
    got(R1M, xh(xp, c, 0))
    send(SX + 4, xh(xp, c, 0), sib)

    @pl.when(native)
    def _():
        load_w.wait()

    @pl.when(foreign)
    def _():
        bundle()
        got(CN, cnt)
        for i in (WYP, WYM, WY2):
            for m in range(3):
                got(i + m, wpart(wq, m))

    def step(k, carry):
        @pl.when(k == 3)
        def _():
            got(SX, xh(x, 1 - c, 0))
            got(SX + 1, xh(x, 1 - c, 1))

            @pl.when(native)
            def _():
                bundle_on()

        @pl.when(k == 4)
        def _():
            got(SX + 2, xh(xm, 1 - c, 0))
            got(SX + 3, xh(xm, 1 - c, 1))

        @pl.when(k == 5)
        def _():
            got(SX + 4, xh(xp, 1 - c, 0))
            got(SX + 5, xh(xp, 1 - c, 1))

        @pl.when(k == 6)
        def _():
            got(R2P, xh(x2, c, 0))
            send(SX + 6, xh(x2, c, 0), sib)
            got(R2M, xh(x2, c, 1))
            send(SX + 7, xh(x2, c, 1), sib)

        @pl.when(k == 7)
        def _():
            got(SX + 6, xh(x2, 1 - c, 0))
            got(SX + 7, xh(x2, 1 - c, 1))

        last = k // 6
        r = lax.rem(k, 3)
        dx = (1 - last) * (r * 3 - (r // 2) * 5) + last * 2
        dp = (1 - last) * (k // 3) + last * (k - 6)
        bx, bp = lax.rem(x + dx, 4), lax.rem(c + dp, 2)
        rows = xg[bx, bp].reshape(ROWS, D)
        at = pl.ds(pl.multiple_of((bx * 2 + bp) * ROWS, ROWS), ROWS)
        for m in range(3):
            qkv[m, at, :] = jnp.dot(rows, wq[m], preferred_element_type=jnp.float32).astype(jnp.bfloat16)
        return carry

    lax.fori_loop(0, 8, step, 0)

    @pl.when(foreign)
    def _():
        bundle_on()

    mine = x * 2 + c
    start = cnt[0:1, 0:1]
    scale = HD**-0.5
    for i in range(8):
        width = (i + 1) * ROWS
        row = i * ROWS + lax.broadcasted_iota(jnp.int32, (ROWS, 1), 0)
        col = lax.broadcasted_iota(jnp.int32, (ROWS, width), 1)
        low = jnp.where(row >= start, start, 0)
        allowed = jnp.logical_and(col >= low, col <= row)
        for hd in range(2):
            lanes = slice(hd * HD, (hd + 1) * HD)
            q = qkv[0, i * ROWS : width, lanes]
            scores = lax.dot_general(
                q, qkv[1, :width, lanes], (((1,), (1,)), ((), ())), preferred_element_type=jnp.float32
            )
            scores = jnp.where(allowed, scores, -1e30)
            highest = jnp.max(scores, axis=1, keepdims=True)
            raised = jnp.exp((scores - highest) * scale)
            total = jnp.sum(raised, axis=1, keepdims=True)
            o = jnp.dot(raised.astype(jnp.bfloat16), qkv[2, :width, lanes], preferred_element_type=jnp.float32)
            obuf[i, :, lanes] = (o / total).astype(jnp.bfloat16)
        bx, bz = i // 2, i % 2
        home = jnp.logical_and(jnp.logical_and(x == bx, s == bz), native)
        owner = place(bx, y, bz * 4 + zl, s)

        @pl.when(home)
        def _():
            mix[mine] = obuf[i]

        @pl.when(jnp.logical_not(home))
        def _():
            pltpu.make_async_remote_copy(
                src_ref=obuf.at[i], dst_ref=mix.at[mine], send_sem=osend.at[i], recv_sem=orecv.at[mine],
                device_id=owner, device_id_type=MESH,
            ).start()

    got(V2P, vlo(y2))
    send(SV + 6, vlo(y2), sib)
    got(V2M, vhi(y2))
    send(SV + 7, vhi(y2), sib)
    for by, i in ((y, 0), (ym, 2), (yp, 4), (y2, 6)):
        got(SV + i, vg.at[pl.ds(0, 2), 1 - c, by])
        got(SV + i + 1, vg.at[pl.ds(2, 2), 1 - c, by])

    for g in range(8):
        here = jnp.logical_and(native, mine == g)

        @pl.when(jnp.logical_not(here))
        def _():
            pltpu.make_async_remote_copy(
                src_ref=mix.at[g], dst_ref=mix.at[g], send_sem=osend.at[0], recv_sem=orecv.at[g],
                device_id=sib, device_id_type=MESH,
            ).wait_recv()

    mixed = jnp.concatenate([mix[g] for g in range(8)], axis=1)
    chunk = 512

    def store(n):
        at = pl.ds(pl.multiple_of(n * chunk, chunk), chunk)
        return pltpu.make_async_copy(obf.at[:, at], out_hbm.at[:, at], outsem.at[n])

    def project(n, carry):
        at = pl.ds(pl.multiple_of(n * chunk, chunk), chunk)
        weight = vg[:, :, :, :, at].reshape(TOTAL, chunk)
        obf[:, at] = jnp.dot(mixed, weight, preferred_element_type=jnp.float32).astype(jnp.bfloat16)
        store(n).start()
        return carry

    lax.fori_loop(0, D // chunk, project, 0)

    for i in range(2):
        for j in (R1P, R1M, SX, SX + 2, SX + 4, SX + 6):
            sent(j + i, xh(x, c, i))
        for j in (V1P, V1M, SV, SV + 2, SV + 4, SV + 6):
            sent(j + i, vlo(y))
    for j in (R2P, R2M):
        sent(j, xh(x, c, 0))
    for j in (V2P, V2M):
        sent(j, vlo(y))
    for j in (WXP, WXM, WX2):
        sent(j, vmine)

    @pl.when(native)
    def _():
        sent(CN, cnt)

    @pl.when(foreign)
    def _():
        for i in range(2):
            sent(ZX + i, xh(x, c, i))
        for j in (WYP, WYM, WY2):
            for m in range(3):
                sent(j + m, wpart(wq, m))

    @pl.when(edge)
    def _():
        for m in range(3):
            sent(WZ + m, wpart(wq, m))
        sent(WZ + 3, vmine)

    for i in range(8):
        bx, bz = i // 2, i % 2
        home = jnp.logical_and(jnp.logical_and(x == bx, s == bz), native)

        @pl.when(jnp.logical_not(home))
        def _():
            pltpu.make_async_remote_copy(
                src_ref=obuf.at[i], dst_ref=mix.at[i], send_sem=osend.at[i], recv_sem=orecv.at[i],
                device_id=sib, device_id_type=MESH,
            ).wait_send()

    for n in range(D // chunk):
        store(n).wait()


def per_device(sessions, input_weight, output_weight, session_counts):
    return pl.pallas_call(
        kernel,
        out_shape=jax.ShapeDtypeStruct((ROWS, D), jnp.bfloat16),
        in_specs=[pl.BlockSpec(memory_space=pltpu.SMEM)] + [pl.BlockSpec(memory_space=pl.ANY)] * 3,
        out_specs=pl.BlockSpec(memory_space=pl.ANY),
        scratch_shapes=[
            pltpu.VMEM((4, 2, 2, HALF, D), jnp.bfloat16),
            pltpu.VMEM((3, D, COLS), jnp.bfloat16),
            pltpu.VMEM((4, 2, 4, 64, D), jnp.bfloat16),
            pltpu.VMEM((3, TOTAL, COLS), jnp.bfloat16),
            pltpu.VMEM((8, ROWS, COLS), jnp.bfloat16),
            pltpu.VMEM((8, ROWS, COLS), jnp.bfloat16),
            pltpu.VMEM((ROWS, D), jnp.bfloat16),
            pltpu.VMEM((8, 128), jnp.int32),
            pltpu.SemaphoreType.DMA((NCOPY,)),
            pltpu.SemaphoreType.DMA((NCOPY,)),
            pltpu.SemaphoreType.DMA((8,)),
            pltpu.SemaphoreType.DMA((8,)),
            pltpu.SemaphoreType.DMA((4,)),
            pltpu.SemaphoreType.DMA((8,)),
        ],
        compiler_params=pltpu.CompilerParams(
            collective_id=0, has_side_effects=True, vmem_limit_bytes=60 * 2**20
        ),
        name="layer",
    )(session_counts, sessions, input_weight, output_weight)


def solution(mesh):
    in_specs = (P(("users", "heads"), None), P(None, None, "heads"), P("heads", None), P("users"))
    out_specs = P(("users", "heads"), None)
    return jax.shard_map(
        per_device, mesh=mesh, in_specs=in_specs, out_specs=out_specs, check_vma=False
    )
```

```python
import jax
import jax.numpy as jnp
from jax import lax
from jax.experimental import pallas as pl
from jax.experimental.pallas import tpu as pltpu
from jax.sharding import PartitionSpec as P

HD = 128
D = 4096
ROWS = 256
CHUNK = 64
TOTAL = 2048
COLS = 256
MESH = pl.DeviceIdType.MESH
ORDER = (0, 2, 1, 3)

ZX = 0
R1P, R1M = 4, 8
R2 = 12
SX = 16
WZ = 80
W1P, W1M = 88, 94
W2P, W2M = 32, 35
VXP, VXM, VX2 = 46, 47, 48
V1P, V1M = 49, 53
V2P, V2M = 57, 60
SV = 63
CN = 79
SW = 100
VF = 112
VX3 = 113
NCOPY = 114


def place(x, y, z, c):
    x, y, z, c = (lax.rem(x + 4, 4), lax.rem(y + 4, 4), lax.rem(z + 8, 8), lax.rem(c, 2))
    return ((y * 4 + lax.rem(z, 4)) * 2 + c, x * 2 + z // 4)


def kernel(
    cnt_ref, x_hbm, w_hbm, v_hbm, out_hbm,
    xg, wq, wf, vg, qkv, obuf, mix, obf, cnt,
    ssem, rsem, osend, orecv, lsem, outsem,
):
    u, h = lax.axis_index("users"), lax.axis_index("heads")
    x, s, y, zl, c = h // 2, lax.rem(h, 2), u // 8, lax.rem(u // 2, 4), lax.rem(u, 2)
    z = s * 4 + zl
    native = c == s
    foreign = c != s
    xm, xp, x2 = lax.rem(x + 3, 4), lax.rem(x + 1, 4), lax.rem(x + 2, 4)
    ym, yp, y2 = lax.rem(y + 3, 4), lax.rem(y + 1, 4), lax.rem(y + 2, 4)
    sib = place(x, y, z, c + 1)
    to_xp, to_xm, to_x2 = place(xp, y, z, c), place(xm, y, z, c), place(x2, y, z, c)
    to_yp, to_ym = place(x, yp, z, c), place(x, ym, z, c)
    across = place(x, y, z + 4, c + 1)
    up, down = place(x, y, z + 1, c), place(x, y, z + 7, c)
    border = place(x, y, z + jnp.where(zl == 3, 1, 7), c + 1)

    def copy(i, src, dst, target):
        return pltpu.make_async_remote_copy(
            src_ref=src, dst_ref=dst, send_sem=ssem.at[i], recv_sem=rsem.at[i],
            device_id=target, device_id_type=MESH,
        )

    def send(i, ref, target):
        copy(i, ref, ref, target).start()

    def got(i, ref):
        copy(i, ref, ref, sib).wait_recv()

    def sent(i, ref):
        copy(i, ref, ref, sib).wait_send()

    def xc(p, j, bx):
        return xg.at[p, j, bx]

    def wp(m, by, ref=None):
        return (wf if ref is None else ref).at[m, pl.ds(pl.multiple_of(by * 1024, 1024), 1024)]

    def wh(m, by, half):
        return wf.at[m, pl.ds(pl.multiple_of(by * 1024 + half * 512, 512), 512)]

    def vp(bx, by):
        return vg.at[bx, c, by]

    def vh(bx, by, half):
        return vg.at[bx, c, by, pl.ds(half * 32, 32)]

    vmine = vp(x, y)
    quarter = v_hbm.at[pl.ds(pl.multiple_of(y * CHUNK, CHUNK), CHUNK)]

    load_x = [
        pltpu.make_async_copy(x_hbm.at[pl.ds(CHUNK * j, CHUNK)], xc(c, j, x), lsem.at[j]) for j in range(4)
    ]
    load_v = [
        pltpu.make_async_copy(v_hbm.at[pl.ds(CHUNK * j, CHUNK)], vg.at[x, s, j], lsem.at[4 + j])
        for j in range(4)
    ]
    load_w = pltpu.make_async_copy(w_hbm, wq, lsem.at[8])

    @pl.when(native)
    def _():
        for cp in load_x:
            cp.start()
        cnt[...] = jnp.full(cnt.shape, cnt_ref[0], jnp.int32)

    for cp in load_v:
        cp.start()

    @pl.when(native)
    def _():
        load_w.start()

    barrier = pltpu.get_barrier_semaphore()
    peers = [place(x + dx, y, z + dz, c + dc) for dx in range(4) for dz in (0, 4) for dc in (0, 1)][1:]
    peers += [to_yp, to_ym, up, down, place(x, y, z + 1, c + 1), place(x, y, z + 7, c + 1)]
    for peer in peers:
        pl.semaphore_signal(barrier, inc=1, device_id=peer, device_id_type=MESH)
    pl.semaphore_wait(barrier, len(peers))

    def first(j):
        send(R1P + j, xc(c, j, x), to_xp)
        send(R1M + j, xc(c, j, x), to_xm)
        send(SX + j, xc(c, j, x), sib)

    def ring(j):
        got(R1P + j, xc(c, j, xm))
        if j < 2:
            send(R2 + j, xc(c, j, xm), to_xp)
        send(SX + 4 + j, xc(c, j, xm), sib)
        got(R1M + j, xc(c, j, xp))
        if j >= 2:
            send(R2 + j, xc(c, j, xp), to_xm)
        send(SX + 8 + j, xc(c, j, xp), sib)

    def tail(j):
        got(R2 + j, xc(c, j, x2))
        send(SX + 12 + j, xc(c, j, x2), sib)

    def from_sib(j):
        for i, bx in enumerate((x, xm, xp, x2)):
            got(SX + 4 * i + j, xc(1 - c, j, bx))

    def share_v():
        send(VXP, vmine, to_xp)
        send(VXM, vmine, to_xm)

    def along_y(q, bx):
        send(V1P + q, vp(bx, y), to_yp)
        send(V1M + q, vp(bx, y), to_ym)
        if q:
            send(SV + q, vp(bx, y), sib)

    def gather_v():
        got(VXP, vp(xm, y))
        send(VX2, vh(xm, y, 0), to_xp)
        along_y(1, xm)
        got(VXM, vp(xp, y))
        send(VX3, vh(xp, y, 1), to_xm)
        along_y(2, xp)

    def gather_v2():
        got(VX2, vh(x2, y, 0))
        got(VX3, vh(x2, y, 1))
        along_y(3, x2)

    def forward_v(own):
        for q, bx in ((1, xm), (2, xp), (3, x2)) + (((0, x),) if own else ()):
            got(V1P + q, vp(bx, ym))
            if q == 1:
                send(V2P, vp(bx, ym), to_yp)
            if q in (0, 3):
                send(V2P + 1 + q // 3, vh(bx, ym, 0), to_yp)
            send(SV + 4 + q, vp(bx, ym), sib)
            got(V1M + q, vp(bx, yp))
            if q == 2:
                send(V2M, vp(bx, yp), to_ym)
            if q in (0, 3):
                send(V2M + 1 + q // 3, vh(bx, yp, 1), to_ym)
            send(SV + 8 + q, vp(bx, yp), sib)

    def last_v(own):
        got(V2P, vp(xm, y2))
        send(SV + 12 + 1, vp(xm, y2), sib)
        got(V2M, vp(xp, y2))
        send(SV + 12 + 2, vp(xp, y2), sib)
        for q, bx in ((3, x2),) + (((0, x),) if own else ()):
            got(V2P + 1 + q // 3, vh(bx, y2, 0))
            got(V2M + 1 + q // 3, vh(bx, y2, 1))
            send(SV + 12 + q, vp(bx, y2), sib)

    def across_z(j):
        copy(ZX + j, x_hbm.at[pl.ds(CHUNK * j, CHUNK)], xc(1 - c, j, x), across).start()

    def piece(m, half):
        return vg.at[x, 1 - c, y, pl.ds(half * 32, 32)] if m == 3 else wh(m, y, half)

    near = zl // 2
    near_to, far_to = place(x, y, z + 9 - 2 * near, c), place(x, y, z + 7 + 2 * near, c)

    def along(m, half):
        if m < 3:
            send(W1P + 2 * m + half, wh(m, y, half), to_yp)
            send(W1M + 2 * m + half, wh(m, y, half), to_ym)

    def relay_near(m):
        i, ref = WZ + 4 * near + m, piece(m, near)
        got(i, ref)
        send(i, ref, near_to)
        along(m, near)

    def relay_far(m):
        i, ref = WZ + 4 * (1 - near) + m, piece(m, 1 - near)
        got(i, ref)

        @pl.when(jnp.logical_or(zl == 1, zl == 2))
        def _():
            send(i, ref, far_to)

        along(m, 1 - near)

    def hand_out(i):
        got(ZX + ORDER[i], xc(c, ORDER[i], x))
        first(ORDER[i])

    def over_border(m, half, i, target):
        if m == 3:
            src = v_hbm.at[pl.ds(pl.multiple_of(y * CHUNK + half * 32, 32), 32)]
            return copy(i + m, src, vh(x, y, half), target)
        src = w_hbm.at[m, pl.ds(pl.multiple_of(y * 1024 + half * 512, 512), 512)]
        return copy(i + m, src, piece(m, half), target)

    def weight_to_sib(i, m, by):
        copy(SW + 3 * i + m, wp(m, by), wp(m, by, wq), sib).start()

    def weights_on(m):
        for half in range(2):
            i = 2 * m + half
            got(W1P + i, wh(m, ym, half))
            if i < 3:
                send(W2P + i, wh(m, ym, half), to_yp)
            got(W1M + i, wh(m, yp, half))
            if i >= 3:
                send(W2M + i - 3, wh(m, yp, half), to_ym)
        weight_to_sib(1, m, ym)
        weight_to_sib(2, m, yp)

    def weights_last():
        for i in range(6):
            got((W2P if i < 3 else W2M - 3) + i, wh(i // 2, y2, i % 2))
            if i % 2:
                weight_to_sib(3, i // 2, y2)

    @pl.when(native)
    def _():
        for edge, half, i in ((3, 0, WZ), (0, 1, WZ + 4)):

            @pl.when(zl == edge)
            def _():
                over_border(0, half, i, border).start()
                over_border(1, half, i, border).start()

        send(CN, cnt, sib)
        for cp in load_x:
            cp.wait()
        for cp in load_v:
            cp.wait()
        share_v()
        for j in ORDER:
            first(j)
        for edge, half, i in ((3, 0, WZ), (0, 1, WZ + 4)):

            @pl.when(zl == edge)
            def _():
                for m in (2, 3):
                    over_border(m - 2, half, i, border).wait_send()
                    over_border(m, half, i, border).start()

        for m in range(4):
            relay_near(m)
        for m in range(4):
            relay_far(m)
        send(VF, vg.at[x, 1 - c, y], sib)
        for m in range(3):
            weight_to_sib(0, m, y)
        gather_v()
        for j in ORDER:
            ring(j)
        for m in range(3):
            weights_on(m)
        gather_v2()
        for j in ORDER:
            tail(j)
        weights_last()
        load_w.wait()

    @pl.when(foreign)
    def _():
        got(VF, vmine)
        across_z(ORDER[0])
        across_z(ORDER[1])
        got(CN, cnt)
        share_v()
        along_y(0, x)
        hand_out(0)
        across_z(ORDER[2])
        gather_v()
        hand_out(1)
        across_z(ORDER[3])
        ring(ORDER[0])
        gather_v2()
        hand_out(2)
        ring(ORDER[1])
        for cp in load_v:
            cp.wait()
        for i, by in enumerate((y, ym, yp, y2)):
            for m in range(3):
                got(SW + 3 * i + m, wp(m, by, wq))

    def step(k, carry):
        for i, j in enumerate(ORDER):

            @pl.when(k == i)
            def _():
                @pl.when(native)
                def _():
                    if i == 3:
                        forward_v(False)

                @pl.when(foreign)
                def _():
                    from_sib(j)
                    if i == 1:
                        hand_out(3)
                        ring(ORDER[2])

            @pl.when(k == 4 + i)
            def _():
                @pl.when(native)
                def _():
                    from_sib(j)

                @pl.when(foreign)
                def _():
                    if i == 2:
                        ring(ORDER[3])
                    tail(j)

        second, r = k // 4, lax.rem(k, 4)
        p = lax.rem(s + second, 2)
        j = (r // 2) + 2 * lax.rem(r, 2)
        rows = xg[p, j].reshape(ROWS, D)
        for m in range(3):
            done = jnp.dot(rows, wq[m], preferred_element_type=jnp.float32).astype(jnp.bfloat16)
            for bx in range(4):
                at = pl.ds(pl.multiple_of((bx * 2 + p) * ROWS + j * CHUNK, CHUNK), CHUNK)
                qkv[m, at, :] = done[bx * CHUNK : (bx + 1) * CHUNK]
        return carry

    lax.fori_loop(0, 8, step, 0)

    @pl.when(foreign)
    def _():
        forward_v(True)

    mine = x * 2 + c
    start = cnt[0:1, 0:1]
    scale = HD**-0.5
    for i in range(8):
        width = (i + 1) * ROWS
        row = i * ROWS + lax.broadcasted_iota(jnp.int32, (ROWS, 1), 0)
        col = lax.broadcasted_iota(jnp.int32, (ROWS, width), 1)
        low = jnp.where(row >= start, start, 0)
        allowed = jnp.logical_and(col >= low, col <= row)
        for hd in range(2):
            lanes = slice(hd * HD, (hd + 1) * HD)
            q = qkv[0, i * ROWS : width, lanes]
            scores = lax.dot_general(
                q, qkv[1, :width, lanes], (((1,), (1,)), ((), ())), preferred_element_type=jnp.float32
            )
            scores = jnp.where(allowed, scores, -1e30)
            highest = jnp.max(scores, axis=1, keepdims=True)
            raised = jnp.exp((scores - highest) * scale)
            total = jnp.sum(raised, axis=1, keepdims=True)
            o = jnp.dot(raised.astype(jnp.bfloat16), qkv[2, :width, lanes], preferred_element_type=jnp.float32)
            obuf[i, :, lanes] = (o / total).astype(jnp.bfloat16)
        bx, bz = i // 2, i % 2
        home = jnp.logical_and(jnp.logical_and(x == bx, s == bz), native)
        owner = place(bx, y, bz * 4 + zl, s)

        @pl.when(home)
        def _():
            mix[mine] = obuf[i]

        @pl.when(jnp.logical_not(home))
        def _():
            pltpu.make_async_remote_copy(
                src_ref=obuf.at[i], dst_ref=mix.at[mine], send_sem=osend.at[i], recv_sem=orecv.at[mine],
                device_id=owner, device_id_type=MESH,
            ).start()

    @pl.when(native)
    def _():
        last_v(False)

    @pl.when(foreign)
    def _():
        last_v(True)

    for i, by in enumerate((y, ym, yp, y2)):
        for q, bx in ((1, xm), (2, xp), (3, x2)):
            got(SV + 4 * i + q, vg.at[bx, 1 - c, by])

        if i:

            @pl.when(native)
            def _():
                got(SV + 4 * i, vg.at[x, 1 - c, by])

    for g in range(8):
        here = jnp.logical_and(native, mine == g)

        @pl.when(jnp.logical_not(here))
        def _():
            pltpu.make_async_remote_copy(
                src_ref=mix.at[g], dst_ref=mix.at[g], send_sem=osend.at[0], recv_sem=orecv.at[g],
                device_id=sib, device_id_type=MESH,
            ).wait_recv()

    mixed = jnp.concatenate([mix[g] for g in range(8)], axis=1)
    chunk = 512

    def store(n):
        at = pl.ds(pl.multiple_of(n * chunk, chunk), chunk)
        return pltpu.make_async_copy(obf.at[:, at], out_hbm.at[:, at], outsem.at[n])

    def project(n, carry):
        at = pl.ds(pl.multiple_of(n * chunk, chunk), chunk)
        weight = vg[:, :, :, :, at].reshape(TOTAL, chunk)
        obf[:, at] = jnp.dot(mixed, weight, preferred_element_type=jnp.float32).astype(jnp.bfloat16)
        store(n).start()
        return carry

    lax.fori_loop(0, D // chunk, project, 0)

    for i in range(4):
        for j in (R1P, R1M, R2, SX, SX + 4, SX + 8, SX + 12):
            sent(j + i, xc(c, i, x))
    for i in range(1, 4):
        for j in (V1P, V1M, SV, SV + 4, SV + 8, SV + 12):
            sent(j + i, vmine)
    for j in (VXP, VXM, V2P, V2M):
        sent(j, vmine)
    for j in (VX2, VX3):
        sent(j, vh(x, y, 0))
    for j in (V2P, V2M):
        sent(j + 2, vh(x, y, 0))

    @pl.when(native)
    def _():
        sent(CN, cnt)
        sent(VF, vmine)
        for i in range(6):
            for j in (W1P, W1M, W2P):
                sent(j + i, wh(0, y, 0))
        for i in range(12):
            sent(SW + i, wp(0, y))
        for m in range(4):
            sent(WZ + 4 * near + m, piece(m, near))

        @pl.when(jnp.logical_or(zl == 1, zl == 2))
        def _():
            for m in range(4):
                sent(WZ + 4 * (1 - near) + m, piece(m, 1 - near))

    @pl.when(foreign)
    def _():
        for i in range(4):
            sent(ZX + i, xc(c, i, x))
        for j in (V1P, V1M, SV + 4, SV + 8, SV + 12):
            sent(j, vmine)
        for j in (V2P, V2M):
            sent(j + 1, vh(x, y, 0))

    for edge, half, i in ((3, 0, WZ), (0, 1, WZ + 4)):

        @pl.when(jnp.logical_and(native, zl == edge))
        def _():
            for m in (2, 3):
                over_border(m, half, i, border).wait_send()

    for i in range(8):
        bx, bz = i // 2, i % 2
        home = jnp.logical_and(jnp.logical_and(x == bx, s == bz), native)

        @pl.when(jnp.logical_not(home))
        def _():
            pltpu.make_async_remote_copy(
                src_ref=obuf.at[i], dst_ref=mix.at[i], send_sem=osend.at[i], recv_sem=orecv.at[i],
                device_id=sib, device_id_type=MESH,
            ).wait_send()

    for n in range(D // chunk):
        store(n).wait()


def per_device(sessions, input_weight, output_weight, session_counts):
    return pl.pallas_call(
        kernel,
        out_shape=jax.ShapeDtypeStruct((ROWS, D), jnp.bfloat16),
        in_specs=[pl.BlockSpec(memory_space=pltpu.SMEM)] + [pl.BlockSpec(memory_space=pl.ANY)] * 3,
        out_specs=pl.BlockSpec(memory_space=pl.ANY),
        scratch_shapes=[
            pltpu.VMEM((2, 4, 4, CHUNK, D), jnp.bfloat16),
            pltpu.VMEM((3, D, COLS), jnp.bfloat16),
            pltpu.VMEM((3, D, COLS), jnp.bfloat16),
            pltpu.VMEM((4, 2, 4, CHUNK, D), jnp.bfloat16),
            pltpu.VMEM((3, TOTAL, COLS), jnp.bfloat16),
            pltpu.VMEM((8, ROWS, COLS), jnp.bfloat16),
            pltpu.VMEM((8, ROWS, COLS), jnp.bfloat16),
            pltpu.VMEM((ROWS, D), jnp.bfloat16),
            pltpu.VMEM((8, 128), jnp.int32),
            pltpu.SemaphoreType.DMA((NCOPY,)),
            pltpu.SemaphoreType.DMA((NCOPY,)),
            pltpu.SemaphoreType.DMA((8,)),
            pltpu.SemaphoreType.DMA((8,)),
            pltpu.SemaphoreType.DMA((9,)),
            pltpu.SemaphoreType.DMA((8,)),
        ],
        compiler_params=pltpu.CompilerParams(
            collective_id=0, has_side_effects=True, vmem_limit_bytes=60 * 2**20
        ),
        name="layer",
    )(session_counts, sessions, input_weight, output_weight)


def solution(mesh):
    in_specs = (P(("users", "heads"), None), P(None, None, "heads"), P("heads", None), P("users"))
    out_specs = P(("users", "heads"), None)
    return jax.shard_map(
        per_device, mesh=mesh, in_specs=in_specs, out_specs=out_specs, check_vma=False
    )
```

```python
import jax
import jax.numpy as jnp
from jax import lax
from jax.experimental import pallas as pl
from jax.experimental.pallas import tpu as pltpu
from jax.sharding import PartitionSpec as P

HD = 128
D = 4096
ROWS = 256
CHUNK = 64
TOTAL = 2048
COLS = 256
MESH = pl.DeviceIdType.MESH
ORDER = (0, 2, 1, 3)

ZX = 0
R1P, R1M = 4, 8
R2 = 12
SX = 16
WZ = 80
W1P, W1M = 88, 94
W2P, W2M = 32, 35
VXP, VXM, VX2 = 46, 47, 48
V1P, V1M = 49, 53
V2P, V2M = 57, 60
SV = 63
CN = 79
SW = 100
VF = 112
VX3 = 113
NCOPY = 114


def place(x, y, z, c):
    x, y, z, c = (lax.rem(x + 4, 4), lax.rem(y + 4, 4), lax.rem(z + 8, 8), lax.rem(c, 2))
    return ((y * 4 + lax.rem(z, 4)) * 2 + c, x * 2 + z // 4)


def kernel(
    cnt_ref, x_hbm, w_hbm, v_hbm, out_hbm,
    xg, wq, wf, vg, qkv, obuf, mix, obf, cnt,
    ssem, rsem, osend, orecv, lsem, outsem,
):
    u, h = lax.axis_index("users"), lax.axis_index("heads")
    x, s, y, zl, c = h // 2, lax.rem(h, 2), u // 8, lax.rem(u // 2, 4), lax.rem(u, 2)
    z = s * 4 + zl
    native = c == s
    foreign = c != s
    xm, xp, x2 = lax.rem(x + 3, 4), lax.rem(x + 1, 4), lax.rem(x + 2, 4)
    ym, yp, y2 = lax.rem(y + 3, 4), lax.rem(y + 1, 4), lax.rem(y + 2, 4)
    sib = place(x, y, z, c + 1)
    to_xp, to_xm, to_x2 = place(xp, y, z, c), place(xm, y, z, c), place(x2, y, z, c)
    to_yp, to_ym = place(x, yp, z, c), place(x, ym, z, c)
    across = place(x, y, z + 4, c + 1)
    up, down = place(x, y, z + 1, c), place(x, y, z + 7, c)
    border = place(x, y, z + jnp.where(zl == 3, 1, 7), c + 1)

    def copy(i, src, dst, target):
        return pltpu.make_async_remote_copy(
            src_ref=src, dst_ref=dst, send_sem=ssem.at[i], recv_sem=rsem.at[i],
            device_id=target, device_id_type=MESH,
        )

    def send(i, ref, target):
        copy(i, ref, ref, target).start()

    def got(i, ref):
        copy(i, ref, ref, sib).wait_recv()

    def sent(i, ref):
        copy(i, ref, ref, sib).wait_send()

    def xc(p, j, bx):
        return xg.at[p, j, bx]

    def wp(m, by, ref=None):
        return (wf if ref is None else ref).at[m, pl.ds(pl.multiple_of(by * 1024, 1024), 1024)]

    def wh(m, by, half):
        return wf.at[m, pl.ds(pl.multiple_of(by * 1024 + half * 512, 512), 512)]

    def vp(bx, by):
        return vg.at[bx, c, by]

    def vh(bx, by, half):
        return vg.at[bx, c, by, pl.ds(half * 32, 32)]

    vmine = vp(x, y)
    quarter = v_hbm.at[pl.ds(pl.multiple_of(y * CHUNK, CHUNK), CHUNK)]

    load_x = [
        pltpu.make_async_copy(x_hbm.at[pl.ds(CHUNK * j, CHUNK)], xc(c, j, x), lsem.at[j]) for j in range(4)
    ]
    load_v = [
        pltpu.make_async_copy(v_hbm.at[pl.ds(CHUNK * j, CHUNK)], vg.at[x, s, j], lsem.at[4 + j])
        for j in range(4)
    ]
    load_w = pltpu.make_async_copy(w_hbm, wq, lsem.at[8])

    @pl.when(native)
    def _():
        for cp in load_x:
            cp.start()
        cnt[...] = jnp.full(cnt.shape, cnt_ref[0], jnp.int32)

    for cp in load_v:
        cp.start()

    @pl.when(native)
    def _():
        load_w.start()

    barrier = pltpu.get_barrier_semaphore()
    peers = [place(x + dx, y, z + dz, c + dc) for dx in range(4) for dz in (0, 4) for dc in (0, 1)][1:]
    peers += [to_yp, to_ym, up, down, place(x, y, z + 1, c + 1), place(x, y, z + 7, c + 1)]
    for peer in peers:
        pl.semaphore_signal(barrier, inc=1, device_id=peer, device_id_type=MESH)
    pl.semaphore_wait(barrier, len(peers))

    def first(j):
        send(R1P + j, xc(c, j, x), to_xp)
        send(R1M + j, xc(c, j, x), to_xm)
        send(SX + j, xc(c, j, x), sib)

    def ring(j):
        got(R1P + j, xc(c, j, xm))
        if j < 2:
            send(R2 + j, xc(c, j, xm), to_xp)
        send(SX + 4 + j, xc(c, j, xm), sib)
        got(R1M + j, xc(c, j, xp))
        if j >= 2:
            send(R2 + j, xc(c, j, xp), to_xm)
        send(SX + 8 + j, xc(c, j, xp), sib)

    def tail(j):
        got(R2 + j, xc(c, j, x2))
        send(SX + 12 + j, xc(c, j, x2), sib)

    def from_sib(j):
        for i, bx in enumerate((x, xm, xp, x2)):
            got(SX + 4 * i + j, xc(1 - c, j, bx))

    def share_v():
        send(VXP, vmine, to_xp)
        send(VXM, vmine, to_xm)

    def along_y(q, bx):
        send(V1P + q, vp(bx, y), to_yp)
        send(V1M + q, vp(bx, y), to_ym)
        if q:
            send(SV + q, vp(bx, y), sib)

    def gather_v():
        got(VXP, vp(xm, y))
        send(VX2, vh(xm, y, 0), to_xp)
        along_y(1, xm)
        got(VXM, vp(xp, y))
        send(VX3, vh(xp, y, 1), to_xm)
        along_y(2, xp)

    def gather_v2():
        got(VX2, vh(x2, y, 0))
        got(VX3, vh(x2, y, 1))
        along_y(3, x2)

    def forward_v(own):
        for q, bx in ((1, xm), (2, xp), (3, x2)) + (((0, x),) if own else ()):
            got(V1P + q, vp(bx, ym))
            if q == 1:
                send(V2P, vp(bx, ym), to_yp)
            if q in (0, 3):
                send(V2P + 1 + q // 3, vh(bx, ym, 0), to_yp)
            send(SV + 4 + q, vp(bx, ym), sib)
            got(V1M + q, vp(bx, yp))
            if q == 2:
                send(V2M, vp(bx, yp), to_ym)
            if q in (0, 3):
                send(V2M + 1 + q // 3, vh(bx, yp, 1), to_ym)
            send(SV + 8 + q, vp(bx, yp), sib)

    def last_v(own):
        got(V2P, vp(xm, y2))
        send(SV + 12 + 1, vp(xm, y2), sib)
        got(V2M, vp(xp, y2))
        send(SV + 12 + 2, vp(xp, y2), sib)
        for q, bx in ((3, x2),) + (((0, x),) if own else ()):
            got(V2P + 1 + q // 3, vh(bx, y2, 0))
            got(V2M + 1 + q // 3, vh(bx, y2, 1))
            send(SV + 12 + q, vp(bx, y2), sib)

    def across_z(j):
        copy(ZX + j, x_hbm.at[pl.ds(CHUNK * j, CHUNK)], xc(1 - c, j, x), across).start()

    def piece(m, half):
        return vg.at[x, 1 - c, y, pl.ds(half * 32, 32)] if m == 3 else wh(m, y, half)

    near = zl // 2
    near_to, far_to = place(x, y, z + 9 - 2 * near, c), place(x, y, z + 7 + 2 * near, c)

    def along(m, half):
        if m < 3:
            send(W1P + 2 * m + half, wh(m, y, half), to_yp)
            send(W1M + 2 * m + half, wh(m, y, half), to_ym)

    def relay_near(m):
        i, ref = WZ + 4 * near + m, piece(m, near)
        got(i, ref)
        send(i, ref, near_to)
        along(m, near)

    def relay_far(m):
        i, ref = WZ + 4 * (1 - near) + m, piece(m, 1 - near)
        got(i, ref)

        @pl.when(jnp.logical_or(zl == 1, zl == 2))
        def _():
            send(i, ref, far_to)

        along(m, 1 - near)

    def hand_out(i):
        got(ZX + ORDER[i], xc(c, ORDER[i], x))
        first(ORDER[i])

    def over_border(m, half, i, target):
        if m == 3:
            src = v_hbm.at[pl.ds(pl.multiple_of(y * CHUNK + half * 32, 32), 32)]
            return copy(i + m, src, vh(x, y, half), target)
        src = w_hbm.at[m, pl.ds(pl.multiple_of(y * 1024 + half * 512, 512), 512)]
        return copy(i + m, src, piece(m, half), target)

    def weight_to_sib(i, m, by):
        copy(SW + 3 * i + m, wp(m, by), wp(m, by, wq), sib).start()

    def weights_on(m):
        for half in range(2):
            i = 2 * m + half
            got(W1P + i, wh(m, ym, half))
            if i < 3:
                send(W2P + i, wh(m, ym, half), to_yp)
            got(W1M + i, wh(m, yp, half))
            if i >= 3:
                send(W2M + i - 3, wh(m, yp, half), to_ym)
        weight_to_sib(1, m, ym)
        weight_to_sib(2, m, yp)

    def weights_last():
        for i in range(6):
            got((W2P if i < 3 else W2M - 3) + i, wh(i // 2, y2, i % 2))
            if i % 2:
                weight_to_sib(3, i // 2, y2)

    @pl.when(native)
    def _():
        for edge, half, i in ((3, 0, WZ), (0, 1, WZ + 4)):

            @pl.when(zl == edge)
            def _():
                over_border(0, half, i, border).start()
                over_border(1, half, i, border).start()

        send(CN, cnt, sib)
        for cp in load_x:
            cp.wait()
        for cp in load_v:
            cp.wait()
        share_v()
        for j in ORDER:
            first(j)
        for edge, half, i in ((3, 0, WZ), (0, 1, WZ + 4)):

            @pl.when(zl == edge)
            def _():
                for m in (2, 3):
                    over_border(m - 2, half, i, border).wait_send()
                    over_border(m, half, i, border).start()

        for m in range(4):
            relay_near(m)
        for m in range(4):
            relay_far(m)
        send(VF, vg.at[x, 1 - c, y], sib)
        for m in range(3):
            weight_to_sib(0, m, y)
        gather_v()
        ring(ORDER[0])
        ring(ORDER[1])
        ring(ORDER[2])
        ring(ORDER[3])
        weights_on(0)
        weights_on(1)
        weights_on(2)
        gather_v2()
        tail(ORDER[0])
        tail(ORDER[1])
        tail(ORDER[2])
        tail(ORDER[3])
        weights_last()
        load_w.wait()

    @pl.when(foreign)
    def _():
        got(VF, vmine)
        across_z(ORDER[0])
        across_z(ORDER[1])
        got(CN, cnt)
        share_v()
        along_y(0, x)
        gather_v()
        hand_out(0)
        across_z(ORDER[2])
        hand_out(1)
        across_z(ORDER[3])
        gather_v2()
        ring(ORDER[0])
        hand_out(2)
        ring(ORDER[1])
        for cp in load_v:
            cp.wait()
        for i, by in enumerate((y, ym, yp, y2)):
            for m in range(3):
                got(SW + 3 * i + m, wp(m, by, wq))

    def step(k, carry):
        for i, j in enumerate(ORDER):

            @pl.when(k == i)
            def _():
                @pl.when(native)
                def _():
                    if i == 3:
                        forward_v(False)

                @pl.when(foreign)
                def _():
                    from_sib(j)
                    if i == 1:
                        hand_out(3)
                        ring(ORDER[2])

            @pl.when(k == 4 + i)
            def _():
                @pl.when(native)
                def _():
                    from_sib(j)

                @pl.when(foreign)
                def _():
                    if i == 0:
                        ring(ORDER[3])
                    tail(j)

        second, r = k // 4, lax.rem(k, 4)
        p = lax.rem(s + second, 2)
        j = (r // 2) + 2 * lax.rem(r, 2)
        rows = xg[p, j].reshape(ROWS, D)
        for m in range(3):
            done = jnp.dot(rows, wq[m], preferred_element_type=jnp.float32).astype(jnp.bfloat16)
            for bx in range(4):
                at = pl.ds(pl.multiple_of((bx * 2 + p) * ROWS + j * CHUNK, CHUNK), CHUNK)
                qkv[m, at, :] = done[bx * CHUNK : (bx + 1) * CHUNK]
        return carry

    lax.fori_loop(0, 8, step, 0)

    @pl.when(foreign)
    def _():
        forward_v(True)

    mine = x * 2 + c
    start = cnt[0:1, 0:1]
    scale = HD**-0.5 * 1.4426950408889634
    for i in range(8):
        width = (i + 1) * ROWS
        row = i * ROWS + lax.broadcasted_iota(jnp.int32, (ROWS, 1), 0)
        col = lax.broadcasted_iota(jnp.int32, (ROWS, width), 1)
        low = jnp.where(row >= start, start, 0)
        allowed = jnp.logical_and(col >= low, col <= row)
        for hd in range(2):
            lanes = slice(hd * HD, (hd + 1) * HD)
            q = qkv[0, i * ROWS : width, lanes]
            scores = lax.dot_general(
                q, qkv[1, :width, lanes], (((1,), (1,)), ((), ())), preferred_element_type=jnp.float32
            )
            scores = jnp.where(allowed, scores, -1e30)
            highest = jnp.max(scores, axis=1, keepdims=True)
            raised = jnp.exp2((scores - highest) * scale)
            total = jnp.sum(raised, axis=1, keepdims=True)
            o = jnp.dot(raised.astype(jnp.bfloat16), qkv[2, :width, lanes], preferred_element_type=jnp.float32)
            obuf[i, :, lanes] = (o / total).astype(jnp.bfloat16)
        bx, bz = i // 2, i % 2
        home = jnp.logical_and(jnp.logical_and(x == bx, s == bz), native)
        owner = place(bx, y, bz * 4 + zl, s)

        @pl.when(home)
        def _():
            mix[mine] = obuf[i]

        @pl.when(jnp.logical_not(home))
        def _():
            pltpu.make_async_remote_copy(
                src_ref=obuf.at[i], dst_ref=mix.at[mine], send_sem=osend.at[i], recv_sem=orecv.at[mine],
                device_id=owner, device_id_type=MESH,
            ).start()

    @pl.when(native)
    def _():
        last_v(False)

    @pl.when(foreign)
    def _():
        last_v(True)

    for i, by in enumerate((y, ym, yp, y2)):
        for q, bx in ((1, xm), (2, xp), (3, x2)):
            got(SV + 4 * i + q, vg.at[bx, 1 - c, by])

        if i:

            @pl.when(native)
            def _():
                got(SV + 4 * i, vg.at[x, 1 - c, by])

    for g in range(8):
        here = jnp.logical_and(native, mine == g)

        @pl.when(jnp.logical_not(here))
        def _():
            pltpu.make_async_remote_copy(
                src_ref=mix.at[g], dst_ref=mix.at[g], send_sem=osend.at[0], recv_sem=orecv.at[g],
                device_id=sib, device_id_type=MESH,
            ).wait_recv()

    mixed = jnp.concatenate([mix[g] for g in range(8)], axis=1)
    chunk = 512

    def store(n):
        at = pl.ds(pl.multiple_of(n * chunk, chunk), chunk)
        return pltpu.make_async_copy(obf.at[:, at], out_hbm.at[:, at], outsem.at[n])

    def project(n, carry):
        at = pl.ds(pl.multiple_of(n * chunk, chunk), chunk)
        weight = vg[:, :, :, :, at].reshape(TOTAL, chunk)
        obf[:, at] = jnp.dot(mixed, weight, preferred_element_type=jnp.float32).astype(jnp.bfloat16)
        store(n).start()
        return carry

    lax.fori_loop(0, D // chunk, project, 0, unroll=True)

    for i in range(4):
        for j in (R1P, R1M, R2, SX, SX + 4, SX + 8, SX + 12):
            sent(j + i, xc(c, i, x))
    for i in range(1, 4):
        for j in (V1P, V1M, SV, SV + 4, SV + 8, SV + 12):
            sent(j + i, vmine)
    for j in (VXP, VXM, V2P, V2M):
        sent(j, vmine)
    for j in (VX2, VX3):
        sent(j, vh(x, y, 0))
    for j in (V2P, V2M):
        sent(j + 2, vh(x, y, 0))

    @pl.when(native)
    def _():
        sent(CN, cnt)
        sent(VF, vmine)
        for i in range(6):
            for j in (W1P, W1M, W2P):
                sent(j + i, wh(0, y, 0))
        for i in range(12):
            sent(SW + i, wp(0, y))
        for m in range(4):
            sent(WZ + 4 * near + m, piece(m, near))

        @pl.when(jnp.logical_or(zl == 1, zl == 2))
        def _():
            for m in range(4):
                sent(WZ + 4 * (1 - near) + m, piece(m, 1 - near))

    @pl.when(foreign)
    def _():
        for i in range(4):
            sent(ZX + i, xc(c, i, x))
        for j in (V1P, V1M, SV + 4, SV + 8, SV + 12):
            sent(j, vmine)
        for j in (V2P, V2M):
            sent(j + 1, vh(x, y, 0))

    for edge, half, i in ((3, 0, WZ), (0, 1, WZ + 4)):

        @pl.when(jnp.logical_and(native, zl == edge))
        def _():
            for m in (2, 3):
                over_border(m, half, i, border).wait_send()

    for i in range(8):
        bx, bz = i // 2, i % 2
        home = jnp.logical_and(jnp.logical_and(x == bx, s == bz), native)

        @pl.when(jnp.logical_not(home))
        def _():
            pltpu.make_async_remote_copy(
                src_ref=obuf.at[i], dst_ref=mix.at[i], send_sem=osend.at[i], recv_sem=orecv.at[i],
                device_id=sib, device_id_type=MESH,
            ).wait_send()

    for n in range(D // chunk):
        store(n).wait()


def per_device(sessions, input_weight, output_weight, session_counts):
    return pl.pallas_call(
        kernel,
        out_shape=jax.ShapeDtypeStruct((ROWS, D), jnp.bfloat16),
        in_specs=[pl.BlockSpec(memory_space=pltpu.SMEM)] + [pl.BlockSpec(memory_space=pl.ANY)] * 3,
        out_specs=pl.BlockSpec(memory_space=pl.ANY),
        scratch_shapes=[
            pltpu.VMEM((2, 4, 4, CHUNK, D), jnp.bfloat16),
            pltpu.VMEM((3, D, COLS), jnp.bfloat16),
            pltpu.VMEM((3, D, COLS), jnp.bfloat16),
            pltpu.VMEM((4, 2, 4, CHUNK, D), jnp.bfloat16),
            pltpu.VMEM((3, TOTAL, COLS), jnp.bfloat16),
            pltpu.VMEM((8, ROWS, COLS), jnp.bfloat16),
            pltpu.VMEM((8, ROWS, COLS), jnp.bfloat16),
            pltpu.VMEM((ROWS, D), jnp.bfloat16),
            pltpu.VMEM((8, 128), jnp.int32),
            pltpu.SemaphoreType.DMA((NCOPY,)),
            pltpu.SemaphoreType.DMA((NCOPY,)),
            pltpu.SemaphoreType.DMA((8,)),
            pltpu.SemaphoreType.DMA((8,)),
            pltpu.SemaphoreType.DMA((9,)),
            pltpu.SemaphoreType.DMA((8,)),
        ],
        compiler_params=pltpu.CompilerParams(
            collective_id=0, has_side_effects=True, vmem_limit_bytes=60 * 2**20
        ),
        name="layer",
    )(session_counts, sessions, input_weight, output_weight)


def solution(mesh):
    in_specs = (P(("users", "heads"), None), P(None, None, "heads"), P("heads", None), P("users"))
    out_specs = P(("users", "heads"), None)
    return jax.shard_map(
        per_device, mesh=mesh, in_specs=in_specs, out_specs=out_specs, check_vma=False
    )
```
